32 devices in a mesh: rows: 8 (over z, y), cols: 4 (over x, core).
Axes of the slice: x: 2, y: 2, z: 4, core: 2. Of those that a mesh axis runs over, the one named last changes fastest.
Arguments:
- features: bfloat16 [4, 64, 640, 128], P(None, 'rows', 'cols'), may hold values from -60 to 60
- conv_first: bfloat16 [3, 3, 3, 128, 128], replicated, may hold values from -0.109375 to 0.109375
- first_reduce_kernel: bfloat16 [3, 3, 128, 256], replicated, may hold values from -0.1875 to 0.1875
- conv_second: bfloat16 [3, 3, 3, 256, 256], replicated, may hold values from -0.078125 to 0.078125
- second_reduce_kernel: bfloat16 [3, 3, 256, 512], replicated, may hold values from -0.125 to 0.125
- conv_last: bfloat16 [3, 3, 3, 512, 32], replicated, may hold values from -0.0546875 to 0.0546875
- gain_first: float32 [128], replicated, may hold values from 0.5 to 1.5
- shift_first: float32 [128], replicated, may hold values from -0.5 to 0.5
- gain_second: float32 [256], replicated, may hold values from 0.5 to 1.5
- shift_second: float32 [256], replicated, may hold values from -0.5 to 0.5
- gain_third: float32 [512], replicated, may hold values from 0.5 to 1.5
- shift_third: float32 [512], replicated, may hold values from -0.5 to 0.5
Outputs:
- moments: bfloat16 [4, 16, 160, 32], P(None, 'rows', 'cols')
The draws below stay inside these ranges and needn't reach their ends.
All inputs are finite; a program needn't handle non-finite values.
Results may differ from the reference program's by a relative error of at most 0.01.
Values may be sent and summed in bfloat16 or wider, within the bound.
A program may use at most 64 MiB of HBM per device.

```python
import jax
import jax.numpy as jnp
from jax import lax

C1 = 128
C2 = 256
C3 = 512
LATENT = 16
GROUPS = 32
FRAMES = 4
HEIGHT = 64
WIDTH = 640


def draw_features(key, part):
    key_base = jax.random.fold_in(key, 11)
    key_cols = jax.random.fold_in(key, 12)
    extent = (FRAMES, HEIGHT, WIDTH, C1)
    row_pos = jnp.arange(HEIGHT, dtype=jnp.float32)
    row_scale = 10.0 ** (row_pos / HEIGHT - 0.5)
    col_scale = 10.0 ** (jax.random.uniform(key_cols, (WIDTH,), jnp.float32) - 0.5)
    base = jax.random.truncated_normal(key_base, -6.0, 6.0, extent, jnp.float32)
    return (base * row_scale[None, :, None, None] * col_scale[None, None, :, None]).astype(jnp.bfloat16)


def gaussian(stream_key, shape, deviation, bound, held_as=jnp.bfloat16):
    return jnp.clip(deviation * jax.random.normal(stream_key, shape, jnp.float32), -bound, bound).astype(held_as)


def setup_inputs(seed: int = 0) -> dict:
    arg_keys = jax.random.split(jax.random.key(seed), 13)
    features = draw_features(jax.random.fold_in(arg_keys[12], 71), 0)
    conv_first = gaussian(arg_keys[1], (3, 3, 3, C1, C1), (27 * C1) ** -0.5, 0.109375)
    first_reduce_kernel = gaussian(arg_keys[2], (3, 3, C1, C2), (9 * C1) ** -0.5, 0.1875)
    conv_second = gaussian(arg_keys[3], (3, 3, 3, C2, C2), (27 * C2) ** -0.5, 0.078125)
    second_reduce_kernel = gaussian(arg_keys[4], (3, 3, C2, C3), (9 * C2) ** -0.5, 0.125)
    conv_last = gaussian(arg_keys[5], (3, 3, 3, C3, 2 * LATENT), (27 * C3) ** -0.5, 0.0546875)
    gain_first = jnp.clip(1.0 + 0.1 * jax.random.normal(arg_keys[6], (C1,), jnp.float32), 0.5, 1.5)
    shift_first = jnp.clip(jax.random.uniform(arg_keys[7], (C1,), jnp.float32, -0.5, 0.5), -0.5, 0.5)
    gain_second = jnp.clip(1.0 + 0.1 * jax.random.normal(arg_keys[8], (C2,), jnp.float32), 0.5, 1.5)
    shift_second = jnp.clip(jax.random.uniform(arg_keys[9], (C2,), jnp.float32, -0.5, 0.5), -0.5, 0.5)
    gain_third = jnp.clip(1.0 + 0.1 * jax.random.normal(arg_keys[10], (C3,), jnp.float32), 0.5, 1.5)
    shift_third = jnp.clip(jax.random.uniform(arg_keys[11], (C3,), jnp.float32, -0.5, 0.5), -0.5, 0.5)
    return {"features": features, "conv_first": conv_first, "first_reduce_kernel": first_reduce_kernel, "conv_second": conv_second, "second_reduce_kernel": second_reduce_kernel, "conv_last": conv_last, "gain_first": gain_first, "shift_first": shift_first, "gain_second": gain_second, "shift_second": shift_second, "gain_third": gain_third, "shift_third": shift_third}


epsilon = 1e-06

def convolve(input_video, weight_tables, strides):
    return lax.conv_general_dilated(input_video[None], weight_tables, strides, 'VALID', dimension_numbers=('NDHWC', 'DHWIO', 'NDHWC'), preferred_element_type=jnp.float32)[0]

def causal_conv(input_video, weight_tables):
    padding = jnp.pad(input_video, ((0, 0), (1, 1), (1, 1), (0, 0)))
    widened = jnp.concatenate([padding[:1], padding[:1], padding], axis=0)
    return convolve(widened, weight_tables, (1, 1, 1))

def norm_silu(values, norm_gain, norm_shift):
    extent = values.shape
    grouped = values.reshape(extent[:3] + (GROUPS, extent[3] // GROUPS))
    mean_value = lax.optimization_barrier(jnp.mean(grouped, axis=(0, 1, 2, 4), keepdims=True))
    variance = lax.optimization_barrier(jnp.mean(jnp.square(grouped - mean_value), axis=(0, 1, 2, 4), keepdims=True))
    result = ((grouped - mean_value) / jnp.sqrt(variance + epsilon)).reshape(extent) * norm_gain + norm_shift
    return jax.nn.silu(result).astype(jnp.bfloat16)

def reduce_resolution(input_video, weight_tables):
    padding = jnp.pad(input_video, ((0, 0), (0, 1), (0, 1), (0, 0)))
    return convolve(padding, weight_tables[None], (1, 2, 2)).astype(jnp.bfloat16)

def reference(features, conv_first, first_reduce_kernel, conv_second, second_reduce_kernel, conv_last, gain_first, shift_first, gain_second, shift_second, gain_third, shift_third):
    hidden_one = causal_conv(features, conv_first)
    first_activation_map = norm_silu(hidden_one, gain_first, shift_first)
    middle_level_features = reduce_resolution(first_activation_map, first_reduce_kernel)
    hidden_two = causal_conv(middle_level_features, conv_second)
    second_activation_map = norm_silu(hidden_two, gain_second, shift_second)
    coarsest_level_features = reduce_resolution(second_activation_map, second_reduce_kernel)
    active_three = norm_silu(coarsest_level_features.astype(jnp.float32), gain_third, shift_third)
    return causal_conv(active_three, conv_last).astype(jnp.bfloat16)
```

```python
import functools

import jax
import jax.numpy as jnp
from jax import lax
from jax.experimental import pallas as pl
from jax.experimental.pallas import tpu as pltpu
from jax.sharding import PartitionSpec as P

GROUPS = 32
EPSILON = 1e-06
LANES = 128
TILE = 8
MESH = pl.DeviceIdType.MESH
F32 = jnp.float32
BF16 = jnp.bfloat16

AROUND = [(-1, 0), (1, 0), (0, -1), (0, 1), (-1, -1), (-1, 1), (1, -1), (1, 1)]
BELOW = [(1, 0), (0, 1), (1, 1)]


def copies_needed(row_peers, col_peers):
    return 2 * len(AROUND) + len(AROUND) + 2 * len(BELOW) + 3 * (row_peers + col_peers - 2)


def packed_type(width):
    return BF16 if width % 16 == 0 else F32


class Net:
    def __init__(self, row_peers, col_peers, send, recv):
        self.row_peers, self.col_peers = row_peers, col_peers
        self.row, self.col = lax.axis_index("rows"), lax.axis_index("cols")
        self.send, self.recv = send, recv
        self.used = 0
        self.pending = []

    def exists(self, dr, dc):
        ok = None
        for place, peers, step in ((self.row, self.row_peers, dr), (self.col, self.col_peers, dc)):
            test = None
            if step < 0:
                test = place > 0
            elif step > 0:
                test = place < peers - 1
            if test is not None:
                ok = test if ok is None else jnp.logical_and(ok, test)
        return ok

    def barrier(self):
        sem = pltpu.get_barrier_semaphore()
        others = [(self.row, lax.rem(self.col + k, self.col_peers)) for k in range(1, self.col_peers)]
        others += [(lax.rem(self.row + k, self.row_peers), self.col) for k in range(1, self.row_peers)]
        others += [
            (
                lax.rem(self.row + dr + self.row_peers, self.row_peers),
                lax.rem(self.col + dc + self.col_peers, self.col_peers),
            )
            for dr, dc in AROUND
            if dr and dc
        ]
        for device in others:
            pl.semaphore_signal(sem, inc=1, device_id=device, device_id_type=MESH)
        pl.semaphore_wait(sem, len(others))

    def halo(self, dr, dc, src, dst):
        slot = self.used
        self.used += 1

        def copy():
            return pltpu.make_async_remote_copy(
                src_ref=src,
                dst_ref=dst,
                send_sem=self.send.at[slot],
                recv_sem=self.recv.at[slot],
                device_id=(self.row - dr, self.col - dc),
                device_id_type=MESH,
            )

        @pl.when(self.exists(-dr, -dc))
        def _():
            copy().start()

        def wait_send():
            @pl.when(self.exists(-dr, -dc))
            def _():
                copy().wait_send()

        return wait_send, lambda: copy().wait_recv()

    def all_sum(self, stat, partial, first, second):
        channels = stat.shape[1]
        total = self.axis_sum(stat, first, self.col_peers, lambda k: (self.row, lax.rem(self.col + k, self.col_peers)))
        partial[...] = total
        return self.axis_sum(partial, second, self.row_peers, lambda k: (lax.rem(self.row + k, self.row_peers), self.col))

    def axis_sum(self, src, slots, peers, device):
        copies = []
        for k in range(1, peers):
            copy = pltpu.make_async_remote_copy(
                src_ref=src,
                dst_ref=slots.at[k - 1],
                send_sem=self.send.at[self.used],
                recv_sem=self.recv.at[self.used],
                device_id=device(k),
                device_id_type=MESH,
            )
            self.used += 1
            copy.start()
            copies.append(copy)
            self.pending.append(copy.wait_send)
        total = src[...]
        for k, copy in enumerate(copies):
            copy.wait_recv()
            total = total + slots[k]
        return total


def group_sums(total):
    channels = total.shape[1]
    shift = (channels // GROUPS).bit_length() - 1
    row = lax.shift_right_logical(lax.broadcasted_iota(jnp.int32, (channels, channels), 0), shift)
    col = lax.shift_right_logical(lax.broadcasted_iota(jnp.int32, (channels, channels), 1), shift)
    same = jnp.where(row == col, 1.0, 0.0).astype(F32)
    return lax.dot_general(
        total, same, (((1,), (0,)), ((), ())),
        precision=lax.Precision.HIGHEST, preferred_element_type=F32,
    )


def norm_terms(total, members, gain):
    sums = group_sums(total) / members
    mean = sums[0:1]
    variance = jnp.maximum(sums[1:2] - mean * mean, 0.0)
    return mean, gain / jnp.sqrt(variance + EPSILON)


def silu_norm(values, mean, factor, shift):
    y = (values - mean) * factor + shift
    return y / (1.0 + jnp.exp(-y))


def clear_rim(buf):
    frames, high, wide, channels = buf.shape
    edge = jnp.zeros((TILE, channels), F32)
    line = jnp.zeros((wide, channels), F32)

    @pl.loop(0, frames)
    def _(t):
        buf[t, 0] = line
        buf[t, high - 1] = line
        for r in range(1, high - 1):
            buf[t, r, pl.ds(0, TILE), :] = edge
            buf[t, r, pl.ds(wide - TILE, TILE), :] = edge


def span(step, length, lead):
    if step < 0:
        return pl.ds(0, lead), pl.ds(length, lead)
    if step > 0:
        return pl.ds(lead + length, lead), pl.ds(lead, lead)
    return pl.ds(lead, length), pl.ds(lead, length)


def start_rim(net, buf, row_sources, row_slots):
    frames, high, wide, channels = buf.shape
    rows, cols = high - 2, wide - 2 * TILE
    parts = []
    for dr, dc in AROUND:
        if dc == 0:
            slot = 0 if dr < 0 else 1
            parts.append((dr, dc) + net.halo(dr, dc, row_sources[slot], row_slots.at[slot]))
            continue
        dst_cols, src_cols = span(dc, cols, TILE)
        dst_rows, src_rows = span(dr, rows, 1)
        parts.append(
            (dr, dc)
            + net.halo(
                dr, dc,
                buf.at[:, src_rows, src_cols, :],
                buf.at[:, dst_rows, dst_cols, :],
            )
        )
    return parts


def finish_rim(net, buf, row_slots, parts, change=None):
    frames, high, wide, channels = buf.shape
    rows, cols = high - 2, wide - 2 * TILE
    for dr, dc, wait_send, wait_recv in parts:
        net.pending.append(wait_send) if change is None else None

        @pl.when(net.exists(dr, dc))
        def _(dr=dr, dc=dc, wait_recv=wait_recv):
            wait_recv()
            if dc == 0:
                slot, place = (0, 0) if dr < 0 else (1, high - 1)

                @pl.loop(0, frames)
                def _(t):
                    value = row_slots[slot, t].astype(F32)
                    buf[t, place, pl.ds(TILE, cols), :] = value if change is None else change(value)
            elif change is not None:
                place_cols, _ = span(dc, cols, TILE)
                lines = range(1, high - 1) if dr == 0 else [0 if dr < 0 else high - 1]

                @pl.loop(0, frames)
                def _(t):
                    for r in lines:
                        buf[t, r, place_cols, :] = change(buf[t, r, place_cols, :])


def gather_taps(buf, taps):
    frames, high, wide, channels = buf.shape
    rows, cols = high - 2, wide - 2 * TILE

    @pl.loop(0, frames)
    def _(t):
        for r in range(high):
            for e in range(3):
                value = buf[t, r, pl.ds(TILE - 1 + e, cols), :].astype(taps.dtype)
                for b in range(3):
                    if 0 <= r - b < rows:
                        taps[t, pl.ds((r - b) * cols, cols), pl.ds((3 * b + e) * channels, channels)] = value


def gather_halved(act, taps):
    frames, high, blocks, wide, lanes = act.shape
    rows, cols = (high - 1) // 2, (wide - TILE) // 2
    channels = blocks * lanes

    @pl.loop(0, frames)
    def _(t):
        for r in range(rows):
            for b in range(3):
                for k in range(blocks):
                    for e in range(3):
                        value = act[t, 2 * r + b, k, pl.ds(e, cols, stride=2), :]
                        taps[t, pl.ds(r * cols, cols), pl.ds((3 * b + e) * channels + k * lanes, lanes)] = (
                            value.astype(taps.dtype)
                        )


def product(left, right):
    return jnp.dot(left.astype(BF16), right, preferred_element_type=F32)


def causal_product(taps, weights, pair, span_rows, emit):
    frames, places = taps.shape[:2]
    channels = weights.shape[2]

    def flat(first, last, places_at):
        value = taps[pl.ds(first, last - first), places_at, :]
        return value.reshape(-1, value.shape[2])

    def stretch(start):
        at = pl.ds(start, span_rows)
        at_frame = lambda value, t: value[t * span_rows : (t + 1) * span_rows]
        last = [None] * frames
        middle = [None] * frames
        oldest = [None] * frames
        if pair is not None:
            both = product(flat(0, frames - 1, at), pair[...])
            for t in range(frames - 1):
                middle[t] = at_frame(both, t)[:, :channels]
                last[t] = at_frame(both, t)[:, channels:]
            last[frames - 1] = product(flat(frames - 1, frames, at), weights[2])
        else:
            both = product(flat(0, frames, at), weights[2])
            last = [at_frame(both, t) for t in range(frames)]
            both = product(flat(0, frames - 1, at), weights[1])
            middle = [at_frame(both, t) for t in range(frames - 1)]
        both = product(flat(0, frames - 2, at), weights[0])
        oldest = [at_frame(both, t) for t in range(frames - 2)]
        emit(start, [
            oldest[max(t - 2, 0)] + middle[max(t - 1, 0)] + last[t] for t in range(frames)
        ])

    steps = places // span_rows
    if steps == 1:
        stretch(0)
    else:
        @pl.loop(0, steps)
        def _(step):
            stretch(pl.multiple_of(step * span_rows, span_rows))


def level(net, buf, taps, weights, pair, lines, act, halved, down, stats, members, gain, shift, ready):
    frames, high, blocks, wide, lanes = act.shape
    rows, cols = high - 1, wide - TILE
    stat, partial, first, second = stats
    gather_taps(buf, taps)
    stat[...] = jnp.zeros_like(stat)

    def emit(start, values):
        line = start // cols if isinstance(start, int) else lax.div(start, cols)
        for t, value in enumerate(values):
            stat[0:1] += jnp.sum(value, axis=0, keepdims=True)
            stat[1:2] += jnp.sum(value * value, axis=0, keepdims=True)
            for i in range(lines):
                for k in range(blocks):
                    act[t, line + i, k, pl.ds(0, cols), :] = value[
                        i * cols : (i + 1) * cols, k * lanes : (k + 1) * lanes
                    ]

    ready()
    causal_product(taps, weights, pair, lines * cols, emit)
    parts = []
    for dr, dc in BELOW:
        dst_rows, src_rows = (pl.ds(rows, 1), pl.ds(0, 1)) if dr else (pl.ds(0, rows), pl.ds(0, rows))
        dst_cols, src_cols = (pl.ds(cols, TILE), pl.ds(0, TILE)) if dc else (pl.ds(0, cols), pl.ds(0, cols))
        parts.append((dr, dc) + net.halo(
            dr, dc,
            act.at[:, src_rows, :, src_cols, :],
            act.at[:, dst_rows, :, dst_cols, :],
        ))
    total = net.all_sum(stat, partial, first, second)
    mean, factor = norm_terms(total, members, gain[...])
    bias = shift[...]

    def change(value, k):
        at = slice(k * lanes, (k + 1) * lanes)
        return silu_norm(value, mean[:, at], factor[:, at], bias[:, at])

    for _, _, wait_send, _ in parts:
        wait_send()

    @pl.loop(0, frames)
    def _(t):
        for r in range(rows):
            for k in range(blocks):
                act[t, r, k, pl.ds(0, cols), :] = change(act[t, r, k, pl.ds(0, cols), :], k)

    for dr, dc, _, wait_recv in parts:
        at = pl.ds(cols, TILE) if dc else pl.ds(0, cols)
        size = TILE if dc else cols
        places = [rows] if dr else list(range(rows))
        there = net.exists(dr, dc)

        @pl.when(there)
        def _(at=at, places=places, wait_recv=wait_recv):
            wait_recv()

            @pl.loop(0, frames)
            def _(t):
                for r in places:
                    for k in range(blocks):
                        act[t, r, k, at, :] = change(act[t, r, k, at, :], k)

        @pl.when(jnp.logical_not(there))
        def _(at=at, places=places, size=size):
            @pl.loop(0, frames)
            def _(t):
                for r in places:
                    for k in range(blocks):
                        act[t, r, k, at, :] = jnp.zeros((size, lanes), F32)

    gather_halved(act, halved)


def fill(buf, t, values, row_send):
    frames, high, wide, channels = buf.shape
    rows, cols = high - 2, wide - 2 * TILE
    for r in range(rows):
        value = values[r * cols : (r + 1) * cols].astype(BF16)
        buf[t, r + 1, pl.ds(TILE, cols), :] = value.astype(F32)
        if r == rows - 1:
            row_send[0, t] = value
        if r == 0:
            row_send[1, t] = value


def kernel(
    row_peers, col_peers,
    x, k1, d1, k2, d2, k3, g1, s1, g2, s2, g3, s3, out,
    xv, w1, pair1, v1, w2, v2, w3,
    buf1, taps1, act1, half1, slots1,
    buf2, taps2, act2, half2, sends2, slots2,
    buf3, taps3, sends3, slots3,
    stat1, part1, fa1, sa1, stat2, part2, fa2, sa2, stat3, part3, fa3, sa3,
    load, send, recv,
):
    net = Net(row_peers, col_peers, send, recv)
    frames, rows, cols, c1 = x.shape
    loads = [
        pltpu.make_async_copy(x, xv, load.at[0]),
        pltpu.make_async_copy(k1, w1, load.at[1]),
        pltpu.make_async_copy(k1.at[1], pair1.at[:, pl.ds(0, c1)], load.at[2]),
        pltpu.make_async_copy(k1.at[2], pair1.at[:, pl.ds(c1, c1)], load.at[3]),
        pltpu.make_async_copy(d1, v1, load.at[4]),
        pltpu.make_async_copy(k2, w2, load.at[5]),
        pltpu.make_async_copy(d2, v2, load.at[6]),
        pltpu.make_async_copy(k3, w3, load.at[7]),
    ]
    for copy in loads:
        copy.start()
    for buf in (buf1, buf2, buf3):
        clear_rim(buf)
    loads[0].wait()

    @pl.loop(0, frames)
    def _(t):
        for r in range(rows):
            buf1[t, r + 1, pl.ds(TILE, cols), :] = xv[t, r].astype(F32)

    net.barrier()
    places = float(frames * rows * cols * row_peers * col_peers)
    parts = start_rim(net, buf1, (x.at[:, rows - 1], x.at[:, 0]), slots1)
    finish_rim(net, buf1, slots1, parts)

    def ready1():
        for copy in loads[1:4]:
            copy.wait()

    level(
        net, buf1, taps1, w1, pair1, 2, act1, half1, v1, (stat1, part1, fa1, sa1),
        places * (c1 // GROUPS), g1, s1, ready1,
    )
    loads[4].wait()

    @pl.loop(0, frames)
    def _(t):
        fill(buf2, t, product(half1[t], v1[...]), sends2)

    parts = start_rim(net, buf2, (sends2.at[0], sends2.at[1]), slots2)
    finish_rim(net, buf2, slots2, parts)
    c2, c3 = v1.shape[1], v2.shape[1]
    level(
        net, buf2, taps2, w2, None, 2, act2, half2, v2, (stat2, part2, fa2, sa2),
        places / 4 * (c2 // GROUPS), g2, s2, loads[5].wait,
    )
    loads[6].wait()
    stat3[...] = jnp.zeros_like(stat3)

    @pl.loop(0, frames)
    def _(t):
        value = product(half2[t], v2[...])
        fill(buf3, t, value, sends3)
        value = value.astype(BF16).astype(F32)
        stat3[0:1] += jnp.sum(value, axis=0, keepdims=True)
        stat3[1:2] += jnp.sum(value * value, axis=0, keepdims=True)

    parts = start_rim(net, buf3, (sends3.at[0], sends3.at[1]), slots3)
    total = net.all_sum(stat3, part3, fa3, sa3)
    mean, factor = norm_terms(total, places / 16 * (c3 // GROUPS), g3[...])
    bias = s3[...]
    change = lambda value: silu_norm(value, mean, factor, bias)
    for _, _, wait_send, _ in parts:
        wait_send()
    rows3, cols3 = buf3.shape[1] - 2, buf3.shape[2] - 2 * TILE

    @pl.loop(0, frames)
    def _(t):
        for r in range(rows3):
            at = pl.ds(TILE, cols3)
            buf3[t, r + 1, at, :] = change(buf3[t, r + 1, at, :])

    finish_rim(net, buf3, slots3, parts, change)
    gather_taps(buf3, taps3)
    loads[7].wait()

    def emit(start, values):
        for t, value in enumerate(values):
            for r in range(rows3):
                out[t, r] = value[r * cols3 : (r + 1) * cols3].astype(BF16)

    causal_product(taps3, w3, None, rows3 * cols3, emit)
    for wait in net.pending:
        wait()


def shards(row_peers, col_peers, x, k1, d1, k2, d2, k3, g1, s1, g2, s2, g3, s3):
    frames, rows, cols, c1 = x.shape
    c2, c3, latent = d1.shape[3], d2.shape[3], k3.shape[4]
    channels = (c1, c2, c3)
    shapes = [(rows >> i, cols >> i) for i in range(3)]
    flat3 = lambda k: k.reshape(3, 9 * k.shape[3], k.shape[4])
    flat2 = lambda k: k.reshape(9 * k.shape[2], k.shape[3])
    weights = (flat3(k1), flat2(d1), flat3(k2), flat2(d2), flat3(k3))
    k1f, d1f, k2f, d2f, k3f = weights

    def padded(i):
        h, w = shapes[i]
        return pltpu.VMEM((frames, h + 2, w + 2 * TILE, channels[i]), F32)

    def taps(i):
        h, w = shapes[i]
        return pltpu.VMEM((frames, h * w, 9 * channels[i]), packed_type(w))

    def act(i):
        h, w = shapes[i]
        return pltpu.VMEM((frames, h + 1, channels[i] // LANES, w + TILE, LANES), F32)

    def half(i):
        h, w = shapes[i + 1]
        return pltpu.VMEM((frames, h * w, 9 * channels[i]), packed_type(w))

    def lines(i):
        return pltpu.VMEM((2, frames, shapes[i][1], channels[i]), BF16)

    def stats(i):
        c = channels[i]
        return [
            pltpu.VMEM((TILE, c), F32),
            pltpu.VMEM((TILE, c), F32),
            pltpu.VMEM((col_peers - 1, TILE, c), F32),
            pltpu.VMEM((row_peers - 1, TILE, c), F32),
        ]

    count = copies_needed(row_peers, col_peers)
    scratch = [
        pltpu.VMEM(x.shape, BF16),
        pltpu.VMEM(k1f.shape, BF16),
        pltpu.VMEM((k1f.shape[1], 2 * c1), BF16),
        pltpu.VMEM(d1f.shape, BF16),
        pltpu.VMEM(k2f.shape, BF16),
        pltpu.VMEM(d2f.shape, BF16),
        pltpu.VMEM(k3f.shape, BF16),
        padded(0), taps(0), act(0), half(0), lines(0),
        padded(1), taps(1), act(1), half(1), lines(1), lines(1),
        padded(2), taps(2), lines(2), lines(2),
        *stats(0), *stats(1), *stats(2),
        pltpu.SemaphoreType.DMA((8,)),
        pltpu.SemaphoreType.DMA((count,)),
        pltpu.SemaphoreType.DMA((count,)),
    ]
    anywhere = pl.BlockSpec(memory_space=pl.ANY)
    local = pl.BlockSpec(memory_space=pltpu.VMEM)
    wide = lambda v: v.reshape(1, -1)
    return pl.pallas_call(
        functools.partial(kernel, row_peers, col_peers),
        out_shape=jax.ShapeDtypeStruct((frames, *shapes[2], latent), BF16),
        in_specs=[anywhere] * 6 + [local] * 6,
        out_specs=local,
        scratch_shapes=scratch,
        compiler_params=pltpu.CompilerParams(
            collective_id=0, has_side_effects=True, vmem_limit_bytes=64000 * 1024
        ),
    )(x, *weights, *map(wide, (g1, s1, g2, s2, g3, s3)))


def solution(mesh):
    block = P(None, "rows", "cols", None)
    body = functools.partial(shards, mesh.shape["rows"], mesh.shape["cols"])
    return jax.shard_map(
        body, mesh=mesh, in_specs=(block,) + (P(),) * 11, out_specs=block, check_vma=False
    )
```

```python
import functools

import jax
import jax.numpy as jnp
from jax import lax
from jax.experimental import pallas as pl
from jax.experimental.pallas import tpu as pltpu
from jax.sharding import PartitionSpec as P

GROUPS = 32
EPSILON = 1e-06
LANES = 128
EDGE = 16
TILE = 8
MESH = pl.DeviceIdType.MESH
F32 = jnp.float32
BF16 = jnp.bfloat16

AROUND = [(-1, 0), (1, 0), (0, -1), (0, 1), (-1, -1), (-1, 1), (1, -1), (1, 1)]
BELOW = [(1, 0), (0, 1), (1, 1)]


def copies_needed(row_peers, col_peers):
    return 2 * len(AROUND) + len(AROUND) + 2 * len(BELOW) + 3 * (row_peers + col_peers - 2)


def packed_type(width):
    return BF16 if width % 16 == 0 else F32


class Net:
    def __init__(self, row_peers, col_peers, send, recv):
        self.row_peers, self.col_peers = row_peers, col_peers
        self.row, self.col = lax.axis_index("rows"), lax.axis_index("cols")
        self.send, self.recv = send, recv
        self.used = 0
        self.pending = []

    def exists(self, dr, dc):
        ok = None
        for place, peers, step in ((self.row, self.row_peers, dr), (self.col, self.col_peers, dc)):
            test = None
            if step < 0:
                test = place > 0
            elif step > 0:
                test = place < peers - 1
            if test is not None:
                ok = test if ok is None else jnp.logical_and(ok, test)
        return ok

    def greet(self):
        sem = pltpu.get_barrier_semaphore()
        others = [(self.row, lax.rem(self.col + k, self.col_peers)) for k in range(1, self.col_peers)]
        others += [(lax.rem(self.row + k, self.row_peers), self.col) for k in range(1, self.row_peers)]
        others += [
            (
                lax.rem(self.row + dr + self.row_peers, self.row_peers),
                lax.rem(self.col + dc + self.col_peers, self.col_peers),
            )
            for dr, dc in AROUND
            if dr and dc
        ]
        for device in others:
            pl.semaphore_signal(sem, inc=1, device_id=device, device_id_type=MESH)
        return lambda: pl.semaphore_wait(sem, len(others))

    def halo(self, dr, dc, src, dst):
        slot = self.used
        self.used += 1

        def copy():
            return pltpu.make_async_remote_copy(
                src_ref=src,
                dst_ref=dst,
                send_sem=self.send.at[slot],
                recv_sem=self.recv.at[slot],
                device_id=(self.row - dr, self.col - dc),
                device_id_type=MESH,
            )

        @pl.when(self.exists(-dr, -dc))
        def _():
            copy().start()

        def wait_send():
            @pl.when(self.exists(-dr, -dc))
            def _():
                copy().wait_send()

        return wait_send, lambda: copy().wait_recv()

    def all_sum(self, groups, stats, between=None, after=None):
        own, partial, first, second = stats
        own[...] = groups
        along = lambda k: (self.row, lax.rem(self.col + k, self.col_peers))
        across = lambda k: (lax.rem(self.row + k, self.row_peers), self.col)
        partial[...] = self.axis_sum(own, first, self.col_peers, along, between)
        return self.axis_sum(partial, second, self.row_peers, across, after)

    def axis_sum(self, src, slots, peers, device, then):
        copies = []
        for k in range(1, peers):
            copy = pltpu.make_async_remote_copy(
                src_ref=src,
                dst_ref=slots.at[k - 1],
                send_sem=self.send.at[self.used],
                recv_sem=self.recv.at[self.used],
                device_id=device(k),
                device_id_type=MESH,
            )
            self.used += 1
            copy.start()
            copies.append(copy)
            self.pending.append(copy.wait_send)
        if then is not None:
            then()
        total = src[...]
        for k, copy in enumerate(copies):
            copy.wait_recv()
            total = total + slots[k]
        return total


def membership(channels, across):
    shape = (channels, LANES) if across else (LANES, channels)
    size = channels // GROUPS
    channel = lax.broadcasted_iota(jnp.int32, shape, 0 if across else 1)
    first = lax.broadcasted_iota(jnp.int32, shape, 1 if across else 0) * size
    return jnp.where(jnp.logical_and(channel >= first, channel < first + size), 1.0, 0.0).astype(F32)


def exact(left, right):
    return lax.dot_general(
        left, right, (((1,), (0,)), ((), ())),
        precision=lax.Precision.HIGHEST, preferred_element_type=F32,
    )


def group_sums(stat):
    return exact(stat[...], membership(stat.shape[1], True))[0:2]


def norm_terms(total, members, gain):
    sums = total / members
    mean = sums[0:1]
    variance = jnp.maximum(sums[1:2] - mean * mean, 0.0)
    inverse = 1.0 / jnp.sqrt(variance + EPSILON)
    first = lax.broadcasted_iota(jnp.int32, (TILE, LANES), 0) == 0
    spread = exact(jnp.where(first, mean, inverse), membership(gain.shape[1], False))
    return spread[0:1], spread[1:2] * gain


def silu_norm(values, mean, factor, shift):
    y = (values - mean) * factor + shift
    return y / (1.0 + jnp.exp(-y))


def clear_rim(buf):
    frames, high, wide, channels = buf.shape
    edge = jnp.zeros((TILE, channels), F32)
    line = jnp.zeros((wide, channels), F32)

    @pl.loop(0, frames)
    def _(t):
        buf[t, 0] = line
        buf[t, high - 1] = line
        for r in range(1, high - 1):
            buf[t, r, pl.ds(0, TILE), :] = edge
            buf[t, r, pl.ds(wide - TILE, TILE), :] = edge


def span(step, length, lead):
    if step < 0:
        return pl.ds(0, lead), pl.ds(length, lead)
    if step > 0:
        return pl.ds(lead + length, lead), pl.ds(lead, lead)
    return pl.ds(lead, length), pl.ds(lead, length)


def start_rim(net, buf, row_sources, row_slots):
    frames, high, wide, channels = buf.shape
    rows, cols = high - 2, wide - 2 * TILE
    parts = []
    for dr, dc in AROUND:
        if dc == 0:
            slot = 0 if dr < 0 else 1
            parts.append((dr, dc) + net.halo(dr, dc, row_sources[slot], row_slots.at[slot]))
            continue
        dst_cols, src_cols = span(dc, cols, TILE)
        dst_rows, src_rows = span(dr, rows, 1)
        parts.append(
            (dr, dc)
            + net.halo(
                dr, dc,
                buf.at[:, src_rows, src_cols, :],
                buf.at[:, dst_rows, dst_cols, :],
            )
        )
    return parts


def finish_rim(net, buf, row_slots, parts, change=None):
    frames, high, wide, channels = buf.shape
    rows, cols = high - 2, wide - 2 * TILE
    for dr, dc, wait_send, wait_recv in parts:
        net.pending.append(wait_send) if change is None else None

        @pl.when(net.exists(dr, dc))
        def _(dr=dr, dc=dc, wait_recv=wait_recv):
            wait_recv()
            if dc == 0:
                slot, place = (0, 0) if dr < 0 else (1, high - 1)

                @pl.loop(0, frames)
                def _(t):
                    value = row_slots[slot, t].astype(F32)
                    buf[t, place, pl.ds(TILE, cols), :] = value if change is None else change(value)
            elif change is not None:
                place_cols, _ = span(dc, cols, TILE)
                lines = range(1, high - 1) if dr == 0 else [0 if dr < 0 else high - 1]

                @pl.loop(0, frames)
                def _(t):
                    for r in lines:
                        buf[t, r, place_cols, :] = change(buf[t, r, place_cols, :])


def gather_taps(buf, taps, lines, spare):
    frames, high, wide, channels = buf.shape
    rows, cols = high - 2, wide - 2 * TILE

    @pl.loop(0, frames)
    def _(t):
        for r in lines:
            for e in range(3):
                start = spare if e == 0 else 0
                size = cols if e == 1 else cols - spare
                value = buf[t, r, pl.ds(TILE - 1 + e + start, size), :].astype(taps.dtype)
                for b in range(3):
                    if 0 <= r - b < rows:
                        put_taps(taps, t, r - b, start, size, 3 * b + e, value)


def put_taps(taps, t, row, start, size, tap, value):
    channels = value.shape[1]
    taps[t, row, pl.ds(start, size), pl.ds(tap * channels, channels)] = value


def patch_taps(buf, taps):
    frames, high, wide, channels = buf.shape
    rows, cols = high - 2, wide - 2 * TILE

    @pl.loop(0, frames)
    def _(t):
        for r in range(1, high - 1):
            for e, start in ((0, 0), (2, cols - EDGE)):
                value = buf[t, r, pl.ds(TILE - 1 + e + start, EDGE), :].astype(taps.dtype)
                for b in range(3):
                    if 0 <= r - b < rows:
                        put_taps(taps, t, r - b, start, EDGE, 3 * b + e, value)


def gather_halved(act, taps):
    frames, high, blocks, wide, lanes = act.shape
    rows, cols = (high - 1) // 2, (wide - TILE) // 2
    channels = blocks * lanes

    @pl.loop(0, frames)
    def _(t):
        for r in range(rows):
            for b in range(3):
                for k in range(blocks):
                    for e in range(3):
                        value = act[t, 2 * r + b, k, pl.ds(e, cols, stride=2), :]
                        taps[t, pl.ds(r * cols, cols), pl.ds((3 * b + e) * channels + k * lanes, lanes)] = (
                            value.astype(taps.dtype)
                        )


def product(left, right):
    return jnp.dot(left.astype(BF16), right, preferred_element_type=F32)


def causal_product(taps, weights, pair, block):
    row, row_count, col, col_count = block
    frames = taps.shape[0]
    channels = weights.shape[2]
    size = row_count * col_count

    def flat(first, last):
        value = taps[pl.ds(first, last - first), pl.ds(row, row_count), pl.ds(col, col_count), :]
        return value.reshape(-1, value.shape[3])

    def split(value):
        return [value[t : t + size] for t in range(0, value.shape[0], size)]

    if pair is not None:
        both = split(product(flat(0, frames - 1), pair[...]))
        middle = [value[:, :channels] for value in both]
        last = [value[:, channels:] for value in both]
        last += split(product(flat(frames - 1, frames), weights[2]))
    else:
        last = split(product(flat(0, frames), weights[2]))
        middle = split(product(flat(0, frames - 1), weights[1]))
    oldest = split(product(flat(0, frames - 2), weights[0]))
    return [oldest[max(t - 2, 0)] + middle[max(t - 1, 0)] + last[t] for t in range(frames)]


def level(
    net, buf, taps, weights, pair, blocks_of, act, halved, edges, stat, stats,
    members, gain, shift, ready, rim_cols, rim_rows,
):
    frames, high, blocks, wide, lanes = act.shape
    rows, cols = high - 1, wide - TILE
    edge_send, edge_recv = edges
    stat[...] = jnp.zeros_like(stat)

    def convolve(block):
        row, row_count, col, col_count = block
        for t, value in enumerate(causal_product(taps, weights, pair, block)):
            stat[0:1] += jnp.sum(value, axis=0, keepdims=True)
            stat[1:2] += jnp.sum(value * value, axis=0, keepdims=True)
            for i in range(row_count):
                for k in range(blocks):
                    act[t, row + i, k, pl.ds(col, col_count), :] = value[
                        i * col_count : (i + 1) * col_count, k * lanes : (k + 1) * lanes
                    ]
            if row == 0:
                edge_send[t] = value[:cols].astype(BF16)

    early, middle, late = blocks_of
    gather_taps(buf, taps, range(1, rows + 1), EDGE)
    ready()
    for block in early:
        convolve(block)
    rim_cols()
    patch_taps(buf, taps)
    for block in middle:
        convolve(block)
    rim_rows()
    gather_taps(buf, taps, (0, rows + 1), 0)
    convolve((0, 1, 0, cols))
    row_send, row_recv = net.halo(1, 0, edge_send, edge_recv)
    for block in late:
        convolve(block)
    parts = []

    def between():
        for dr, dc in ((0, 1), (1, 1)):
            dst_rows, src_rows = (pl.ds(rows, 1), pl.ds(0, 1)) if dr else (pl.ds(0, rows), pl.ds(0, rows))
            parts.append((dr, dc) + net.halo(
                dr, dc,
                act.at[:, src_rows, :, pl.ds(0, TILE), :],
                act.at[:, dst_rows, :, pl.ds(cols, TILE), :],
            ))

    total = net.all_sum(group_sums(stat), stats, between)
    mean, factor = norm_terms(total, members, gain[...])
    bias = shift[...]

    def change(value, k):
        at = slice(k * lanes, (k + 1) * lanes)
        return silu_norm(value, mean[:, at], factor[:, at], bias[:, at])

    net.pending.append(row_send)
    for _, _, wait_send, _ in parts:
        wait_send()

    @pl.loop(0, frames)
    def _(t):
        for r in range(rows):
            for k in range(blocks):
                act[t, r, k, pl.ds(0, cols), :] = change(act[t, r, k, pl.ds(0, cols), :], k)

    def border(dr, dc, finish):
        at = pl.ds(cols, TILE) if dc else pl.ds(0, cols)
        size = TILE if dc else cols
        places = [rows] if dr else list(range(rows))
        there = net.exists(dr, dc)

        @pl.when(there)
        def _():
            finish()

            @pl.loop(0, frames)
            def _(t):
                for r in places:
                    for k in range(blocks):
                        if dc:
                            value = act[t, r, k, at, :]
                        else:
                            value = edge_recv[t, :, pl.ds(k * lanes, lanes)].astype(F32)
                        act[t, r, k, at, :] = change(value, k)

        @pl.when(jnp.logical_not(there))
        def _():
            @pl.loop(0, frames)
            def _(t):
                for r in places:
                    for k in range(blocks):
                        act[t, r, k, at, :] = jnp.zeros((size, lanes), F32)

    border(1, 0, row_recv)
    for dr, dc, _, wait_recv in parts:
        border(dr, dc, wait_recv)
    gather_halved(act, halved)


def fill(buf, t, values, row_send):
    frames, high, wide, channels = buf.shape
    rows, cols = high - 2, wide - 2 * TILE
    for r in range(rows):
        value = values[r * cols : (r + 1) * cols].astype(BF16)
        buf[t, r + 1, pl.ds(TILE, cols), :] = value.astype(F32)
        if r == rows - 1:
            row_send[0, t] = value
        if r == 0:
            row_send[1, t] = value


def kernel(
    row_peers, col_peers,
    x, k1, d1, k2, d2, k3, g1, s1, g2, s2, g3, s3, out,
    xv, w1, pair1, v1, w2, v2, w3,
    buf1, taps1, act1, half1, slots1, edge1, edged1,
    buf2, taps2, act2, half2, sends2, slots2, edge2, edged2,
    buf3, taps3, sends3, slots3,
    stat1, own1, part1, fa1, sa1, stat2, own2, part2, fa2, sa2, stat3, own3, part3, fa3, sa3,
    load, send, recv,
):
    net = Net(row_peers, col_peers, send, recv)
    frames, rows, cols, c1 = x.shape
    latent = k3.shape[2]
    loads = [
        pltpu.make_async_copy(x, xv, load.at[0]),
        pltpu.make_async_copy(k1, w1, load.at[1]),
        pltpu.make_async_copy(k1.at[1], pair1.at[:, pl.ds(0, c1)], load.at[2]),
        pltpu.make_async_copy(k1.at[2], pair1.at[:, pl.ds(c1, c1)], load.at[3]),
        pltpu.make_async_copy(d1, v1, load.at[4]),
        pltpu.make_async_copy(k2, w2, load.at[5]),
        pltpu.make_async_copy(d2, v2, load.at[6]),
    ]
    for a in range(3):
        loads.append(pltpu.make_async_copy(k3.at[a], w3.at[:, pl.ds(a * latent, latent), :], load.at[7 + a]))
    for copy in loads:
        copy.start()
    for buf in (buf1, buf2, buf3):
        clear_rim(buf)
    arrive = net.greet()
    loads[0].wait()

    @pl.loop(0, frames)
    def _(t):
        for r in range(rows):
            buf1[t, r + 1, pl.ds(TILE, cols), :] = xv[t, r].astype(F32)

    places = float(frames * rows * cols * row_peers * col_peers)
    held = []
    beside = lambda parts: [part for part in parts if part[0] == 0]
    beyond = lambda parts: [part for part in parts if part[0] != 0]

    def rim_cols1():
        arrive()
        held.extend(start_rim(net, buf1, (x.at[:, rows - 1], x.at[:, 0]), slots1))
        finish_rim(net, buf1, slots1, beside(held))

    def ready1():
        for copy in loads[1:4]:
            copy.wait()

    within = [(1, rows - 2, EDGE, cols - 2 * EDGE)]
    strips = [(1, rows - 2, 0, EDGE), (1, rows - 2, cols - EDGE, EDGE)]
    level(
        net, buf1, taps1, w1, pair1, (within, strips, [(rows - 1, 1, 0, cols)]),
        act1, half1, (edge1, edged1), stat1, (own1, part1, fa1, sa1),
        places * (c1 // GROUPS), g1, s1, ready1,
        rim_cols1, lambda: finish_rim(net, buf1, slots1, beyond(held)),
    )
    loads[4].wait()

    @pl.loop(0, frames)
    def _(t):
        fill(buf2, t, product(half1[t], v1[...]), sends2)

    parts = start_rim(net, buf2, (sends2.at[0], sends2.at[1]), slots2)
    c2, c3 = v1.shape[1], v2.shape[1]
    rows2, cols2 = buf2.shape[1] - 2, buf2.shape[2] - 2 * TILE
    level(
        net, buf2, taps2, w2, None,
        ([], [(1, rows2 - 2, 0, cols2)], [(rows2 - 1, 1, 0, cols2)]),
        act2, half2, (edge2, edged2), stat2, (own2, part2, fa2, sa2),
        places / 4 * (c2 // GROUPS), g2, s2, loads[5].wait,
        lambda: finish_rim(net, buf2, slots2, beside(parts)),
        lambda: finish_rim(net, buf2, slots2, beyond(parts)),
    )
    loads[6].wait()
    stat3[...] = jnp.zeros_like(stat3)

    @pl.loop(0, frames)
    def _(t):
        value = product(half2[t], v2[...])
        fill(buf3, t, value, sends3)
        value = value.astype(BF16).astype(F32)
        stat3[0:1] += jnp.sum(value, axis=0, keepdims=True)
        stat3[1:2] += jnp.sum(value * value, axis=0, keepdims=True)

    rims = []
    total = net.all_sum(
        group_sums(stat3), (own3, part3, fa3, sa3), None,
        lambda: rims.extend(start_rim(net, buf3, (sends3.at[0], sends3.at[1]), slots3)),
    )
    mean, factor = norm_terms(total, places / 16 * (c3 // GROUPS), g3[...])
    bias = s3[...]
    change = lambda value: silu_norm(value, mean, factor, bias)
    for dr, dc, wait_send, _ in rims:
        net.pending.append(wait_send) if dc == 0 else wait_send()
    rows3, cols3 = buf3.shape[1] - 2, buf3.shape[2] - 2 * TILE

    @pl.loop(0, frames)
    def _(t):
        for r in range(rows3):
            at = pl.ds(TILE, cols3)
            buf3[t, r + 1, at, :] = change(buf3[t, r + 1, at, :])

    finish_rim(net, buf3, slots3, rims, change)

    @pl.loop(0, frames)
    def _(t):
        for r in range(rows3 + 2):
            for e in range(3):
                value = buf3[t, r, pl.ds(TILE - 1 + e, cols3), :]
                for b in range(3):
                    if 0 <= r - b < rows3:
                        taps3[t, pl.ds((r - b) * cols3, cols3), pl.ds((3 * b + e) * c3, c3)] = value

    for copy in loads[7:]:
        copy.wait()
    total = None
    for tap in range(9):
        left = taps3[:, :, pl.ds(tap * c3, c3)].reshape(-1, c3).astype(BF16)
        term = lax.dot_general(left, w3[tap], (((1,), (1,)), ((), ())), preferred_element_type=F32)
        total = term if total is None else total + term
    size = rows3 * cols3
    ages = [
        [total[t * size : (t + 1) * size, a * latent : (a + 1) * latent] for t in range(frames)]
        for a in range(3)
    ]
    for t in range(frames):
        value = ages[0][max(t - 2, 0)] + ages[1][max(t - 1, 0)] + ages[2][t]
        for r in range(rows3):
            out[t, r] = value[r * cols3 : (r + 1) * cols3].astype(BF16)
    for wait in net.pending:
        wait()


def shards(row_peers, col_peers, x, k1, d1, k2, d2, k3, g1, s1, g2, s2, g3, s3):
    frames, rows, cols, c1 = x.shape
    c2, c3, latent = d1.shape[3], d2.shape[3], k3.shape[4]
    channels = (c1, c2, c3)
    shapes = [(rows >> i, cols >> i) for i in range(3)]
    flat3 = lambda k: k.reshape(3, 9 * k.shape[3], k.shape[4])
    flat2 = lambda k: k.reshape(9 * k.shape[2], k.shape[3])
    k3 = jnp.swapaxes(k3, 3, 4).reshape(3, 9, latent, c3)
    weights = (flat3(k1), flat2(d1), flat3(k2), flat2(d2), k3)
    k1f, d1f, k2f, d2f, _ = weights

    def padded(i):
        h, w = shapes[i]
        return pltpu.VMEM((frames, h + 2, w + 2 * TILE, channels[i]), F32)

    def taps(i):
        h, w = shapes[i]
        return pltpu.VMEM((frames, h, w, 9 * channels[i]), BF16)

    def last_taps():
        h, w = shapes[2]
        return pltpu.VMEM((frames, h * w, 9 * channels[2]), F32)

    def edge(i):
        return pltpu.VMEM((frames, shapes[i][1], channels[i]), BF16)

    def act(i):
        h, w = shapes[i]
        return pltpu.VMEM((frames, h + 1, channels[i] // LANES, w + TILE, LANES), F32)

    def half(i):
        h, w = shapes[i + 1]
        return pltpu.VMEM((frames, h * w, 9 * channels[i]), packed_type(w))

    def lines(i):
        return pltpu.VMEM((2, frames, shapes[i][1], channels[i]), BF16)

    def stats(i):
        c = channels[i]
        return [
            pltpu.VMEM((TILE, c), F32),
            pltpu.VMEM((2, LANES), F32),
            pltpu.VMEM((2, LANES), F32),
            pltpu.VMEM((col_peers - 1, 2, LANES), F32),
            pltpu.VMEM((row_peers - 1, 2, LANES), F32),
        ]

    count = copies_needed(row_peers, col_peers)
    scratch = [
        pltpu.VMEM(x.shape, BF16),
        pltpu.VMEM(k1f.shape, BF16),
        pltpu.VMEM((k1f.shape[1], 2 * c1), BF16),
        pltpu.VMEM(d1f.shape, BF16),
        pltpu.VMEM(k2f.shape, BF16),
        pltpu.VMEM(d2f.shape, BF16),
        pltpu.VMEM((9, 3 * latent, c3), BF16),
        padded(0), taps(0), act(0), half(0), lines(0), edge(0), edge(0),
        padded(1), taps(1), act(1), half(1), lines(1), lines(1), edge(1), edge(1),
        padded(2), last_taps(), lines(2), lines(2),
        *stats(0), *stats(1), *stats(2),
        pltpu.SemaphoreType.DMA((10,)),
        pltpu.SemaphoreType.DMA((count,)),
        pltpu.SemaphoreType.DMA((count,)),
    ]
    anywhere = pl.BlockSpec(memory_space=pl.ANY)
    local = pl.BlockSpec(memory_space=pltpu.VMEM)
    wide = lambda v: v.reshape(1, -1)
    return pl.pallas_call(
        functools.partial(kernel, row_peers, col_peers),
        out_shape=jax.ShapeDtypeStruct((frames, *shapes[2], latent), BF16),
        in_specs=[anywhere] * 6 + [local] * 6,
        out_specs=local,
        scratch_shapes=scratch,
        compiler_params=pltpu.CompilerParams(
            collective_id=0, has_side_effects=True, vmem_limit_bytes=64000 * 1024
        ),
    )(x, *weights, *map(wide, (g1, s1, g2, s2, g3, s3)))


def solution(mesh):
    block = P(None, "rows", "cols", None)
    body = functools.partial(shards, mesh.shape["rows"], mesh.shape["cols"])
    return jax.shard_map(
        body, mesh=mesh, in_specs=(block,) + (P(),) * 11, out_specs=block, check_vma=False
    )
```

```python
import functools

import jax
import jax.numpy as jnp
from jax import lax
from jax.experimental import pallas as pl
from jax.experimental.pallas import tpu as pltpu
from jax.sharding import PartitionSpec as P

GROUPS = 32
EPSILON = 1e-06
LANES = 128
EDGE = 16
TILE = 8
MESH = pl.DeviceIdType.MESH
F32 = jnp.float32
BF16 = jnp.bfloat16

AROUND = [(-1, 0), (1, 0), (0, -1), (0, 1), (-1, -1), (-1, 1), (1, -1), (1, 1)]
BELOW = [(1, 0), (0, 1), (1, 1)]


def copies_needed(row_peers, col_peers):
    return 2 * len(AROUND) + len(AROUND) + 2 * (len(BELOW) + 1) + 3 * (row_peers + col_peers - 2)


def packed_type(width):
    return BF16 if width % 16 == 0 else F32


class Net:
    def __init__(self, row_peers, col_peers, send, recv):
        self.row_peers, self.col_peers = row_peers, col_peers
        self.row, self.col = lax.axis_index("rows"), lax.axis_index("cols")
        self.send, self.recv = send, recv
        self.used = 0
        self.pending = []

    def exists(self, dr, dc):
        ok = None
        for place, peers, step in ((self.row, self.row_peers, dr), (self.col, self.col_peers, dc)):
            test = None
            if step < 0:
                test = place > 0
            elif step > 0:
                test = place < peers - 1
            if test is not None:
                ok = test if ok is None else jnp.logical_and(ok, test)
        return ok

    def greet(self):
        sem = pltpu.get_barrier_semaphore()
        others = [(self.row, lax.rem(self.col + k, self.col_peers)) for k in range(1, self.col_peers)]
        others += [(lax.rem(self.row + k, self.row_peers), self.col) for k in range(1, self.row_peers)]
        others += [
            (
                lax.rem(self.row + dr + self.row_peers, self.row_peers),
                lax.rem(self.col + dc + self.col_peers, self.col_peers),
            )
            for dr, dc in AROUND
            if dr and dc
        ]
        for device in others:
            pl.semaphore_signal(sem, inc=1, device_id=device, device_id_type=MESH)
        return lambda: pl.semaphore_wait(sem, len(others))

    def halo(self, dr, dc, src, dst):
        slot = self.used
        self.used += 1

        def copy():
            return pltpu.make_async_remote_copy(
                src_ref=src,
                dst_ref=dst,
                send_sem=self.send.at[slot],
                recv_sem=self.recv.at[slot],
                device_id=(self.row - dr, self.col - dc),
                device_id_type=MESH,
            )

        @pl.when(self.exists(-dr, -dc))
        def _():
            copy().start()

        def wait_send():
            @pl.when(self.exists(-dr, -dc))
            def _():
                copy().wait_send()

        return wait_send, lambda: copy().wait_recv()

    def all_sum(self, groups, stats, between=None, after=None):
        own, partial, first, second = stats
        own[...] = groups
        along = lambda k: (self.row, lax.rem(self.col + k, self.col_peers))
        across = lambda k: (lax.rem(self.row + k, self.row_peers), self.col)
        partial[...] = self.axis_sum(own, first, self.col_peers, along, between)
        return self.axis_sum(partial, second, self.row_peers, across, after)

    def axis_sum(self, src, slots, peers, device, then):
        copies = []
        for k in range(1, peers):
            copy = pltpu.make_async_remote_copy(
                src_ref=src,
                dst_ref=slots.at[k - 1],
                send_sem=self.send.at[self.used],
                recv_sem=self.recv.at[self.used],
                device_id=device(k),
                device_id_type=MESH,
            )
            self.used += 1
            copy.start()
            copies.append(copy)
            self.pending.append(copy.wait_send)
        if then is not None:
            then()
        total = src[...]
        for k, copy in enumerate(copies):
            copy.wait_recv()
            total = total + slots[k]
        return total


def membership(channels, across):
    shape = (channels, LANES) if across else (LANES, channels)
    size = channels // GROUPS
    channel = lax.broadcasted_iota(jnp.int32, shape, 0 if across else 1)
    first = lax.broadcasted_iota(jnp.int32, shape, 1 if across else 0) * size
    return jnp.where(jnp.logical_and(channel >= first, channel < first + size), 1.0, 0.0).astype(F32)


def exact(left, right):
    return lax.dot_general(
        left, right, (((1,), (0,)), ((), ())),
        precision=lax.Precision.HIGHEST, preferred_element_type=F32,
    )


def group_sums(stat):
    return exact(stat[...], membership(stat.shape[1], True))[0:2]


def norm_terms(total, members, gain):
    sums = total / members
    mean = sums[0:1]
    variance = jnp.maximum(sums[1:2] - mean * mean, 0.0)
    inverse = 1.0 / jnp.sqrt(variance + EPSILON)
    first = lax.broadcasted_iota(jnp.int32, (TILE, LANES), 0) == 0
    spread = exact(jnp.where(first, mean, inverse), membership(gain.shape[1], False))
    return spread[0:1], spread[1:2] * gain


def silu_norm(values, mean, factor, shift):
    y = (values - mean) * factor + shift
    return y / (1.0 + jnp.exp(-y))


def clear_rim(buf):
    frames, high, wide, channels = buf.shape
    edge = jnp.zeros((TILE, channels), F32)
    line = jnp.zeros((wide, channels), F32)

    @pl.loop(0, frames)
    def _(t):
        buf[t, 0] = line
        buf[t, high - 1] = line
        for r in range(1, high - 1):
            buf[t, r, pl.ds(0, TILE), :] = edge
            buf[t, r, pl.ds(wide - TILE, TILE), :] = edge


def span(step, length, lead):
    if step < 0:
        return pl.ds(0, lead), pl.ds(length, lead)
    if step > 0:
        return pl.ds(lead + length, lead), pl.ds(lead, lead)
    return pl.ds(lead, length), pl.ds(lead, length)


def start_rim(net, buf, row_sources, row_slots):
    frames, high, wide, channels = buf.shape
    rows, cols = high - 2, wide - 2 * TILE
    parts = []
    for dr, dc in AROUND:
        if dc == 0:
            slot = 0 if dr < 0 else 1
            parts.append((dr, dc) + net.halo(dr, dc, row_sources[slot], row_slots.at[slot]))
            continue
        dst_cols, src_cols = span(dc, cols, TILE)
        dst_rows, src_rows = span(dr, rows, 1)
        parts.append(
            (dr, dc)
            + net.halo(
                dr, dc,
                buf.at[:, src_rows, src_cols, :],
                buf.at[:, dst_rows, dst_cols, :],
            )
        )
    return parts


def finish_rim(net, buf, row_slots, parts, change=None):
    frames, high, wide, channels = buf.shape
    rows, cols = high - 2, wide - 2 * TILE
    for dr, dc, wait_send, wait_recv in parts:
        net.pending.append(wait_send) if change is None else None

        @pl.when(net.exists(dr, dc))
        def _(dr=dr, dc=dc, wait_recv=wait_recv):
            wait_recv()
            if dc == 0:
                slot, place = (0, 0) if dr < 0 else (1, high - 1)

                @pl.loop(0, frames)
                def _(t):
                    value = row_slots[slot, t].astype(F32)
                    buf[t, place, pl.ds(TILE, cols), :] = value if change is None else change(value)
            elif change is not None:
                place_cols, _ = span(dc, cols, TILE)
                lines = range(1, high - 1) if dr == 0 else [0 if dr < 0 else high - 1]

                @pl.loop(0, frames)
                def _(t):
                    for r in lines:
                        buf[t, r, place_cols, :] = change(buf[t, r, place_cols, :])


def gather_taps(buf, taps, lines, spare):
    frames, high, wide, channels = buf.shape
    rows, cols = high - 2, wide - 2 * TILE

    @pl.loop(0, frames)
    def _(t):
        for r in lines:
            for e in range(3):
                start = spare if e == 0 else 0
                size = cols if e == 1 else cols - spare
                value = buf[t, r, pl.ds(TILE - 1 + e + start, size), :].astype(taps.dtype)
                for b in range(3):
                    if 0 <= r - b < rows:
                        put_taps(taps, t, r - b, start, size, 3 * b + e, value)


def put_taps(taps, t, row, start, size, tap, value):
    channels = value.shape[1]
    taps[t, row, pl.ds(start, size), pl.ds(tap * channels, channels)] = value


def patch_taps(buf, taps):
    frames, high, wide, channels = buf.shape
    rows, cols = high - 2, wide - 2 * TILE

    @pl.loop(0, frames)
    def _(t):
        for r in range(1, high - 1):
            for e, start in ((0, 0), (2, cols - EDGE)):
                value = buf[t, r, pl.ds(TILE - 1 + e + start, EDGE), :].astype(taps.dtype)
                for b in range(3):
                    if 0 <= r - b < rows:
                        put_taps(taps, t, r - b, start, EDGE, 3 * b + e, value)


def gather_halved(act, taps):
    frames, high, blocks, wide, lanes = act.shape
    rows, cols = (high - 1) // 2, (wide - TILE) // 2
    channels = blocks * lanes

    @pl.loop(0, frames)
    def _(t):
        for r in range(rows):
            for b in range(3):
                for k in range(blocks):
                    for e in range(3):
                        value = act[t, 2 * r + b, k, pl.ds(e, cols, stride=2), :]
                        taps[t, pl.ds(r * cols, cols), pl.ds((3 * b + e) * channels + k * lanes, lanes)] = (
                            value.astype(taps.dtype)
                        )


def product(left, right):
    return jnp.dot(left.astype(BF16), right, preferred_element_type=F32)


def causal_product(taps, weights, pair, block):
    row, row_count, col, col_count = block
    frames = taps.shape[0]
    channels = weights.shape[2]
    size = row_count * col_count

    def flat(first, last):
        value = taps[pl.ds(first, last - first), pl.ds(row, row_count), pl.ds(col, col_count), :]
        return value.reshape(-1, value.shape[3])

    def split(value):
        return [value[t : t + size] for t in range(0, value.shape[0], size)]

    if pair is not None:
        both = split(product(flat(0, frames - 1), pair[...]))
        middle = [value[:, :channels] for value in both]
        last = [value[:, channels:] for value in both]
        last += split(product(flat(frames - 1, frames), weights[2]))
    else:
        last = split(product(flat(0, frames), weights[2]))
        middle = split(product(flat(0, frames - 1), weights[1]))
    oldest = split(product(flat(0, frames - 2), weights[0]))
    return [oldest[max(t - 2, 0)] + middle[max(t - 1, 0)] + last[t] for t in range(frames)]


def level(
    net, buf, taps, weights, pair, blocks_of, act, halved, edges, stat, stats,
    members, gain, shift, ready, rim_cols, rim_rows,
):
    frames, high, blocks, wide, lanes = act.shape
    rows, cols = high - 1, wide - TILE
    edge_send, edge_recv, center_send, center_recv = edges
    stat[...] = jnp.zeros_like(stat)

    def convolve(block):
        row, row_count, col, col_count = block
        for t, value in enumerate(causal_product(taps, weights, pair, block)):
            stat[0:1] += jnp.sum(value, axis=0, keepdims=True)
            stat[1:2] += jnp.sum(value * value, axis=0, keepdims=True)
            for i in range(row_count):
                for k in range(blocks):
                    act[t, row + i, k, pl.ds(col, col_count), :] = value[
                        i * col_count : (i + 1) * col_count, k * lanes : (k + 1) * lanes
                    ]

    early, middle, late = blocks_of
    gather_taps(buf, taps, range(1, rows + 1), EDGE)
    ready()
    for block in early:
        convolve(block)
    rim_cols()
    patch_taps(buf, taps)
    for block in middle:
        convolve(block)
    rim_rows()
    gather_taps(buf, taps, (0, rows + 1), 0)
    for block in late:
        convolve(block)
    parts, lines = [], []

    def between():
        center = stat[0:1] / float(frames * rows * cols)
        center_send[...] = jnp.broadcast_to(center, center_send.shape)

        @pl.loop(0, frames)
        def _(t):
            for k in range(blocks):
                at = slice(k * lanes, (k + 1) * lanes)
                value = act[t, 0, k, pl.ds(0, cols), :] - center[:, at]
                edge_send[t, :, pl.ds(k * lanes, lanes)] = value.astype(BF16)

        for dr, dc in ((0, 1), (1, 1)):
            dst_rows, src_rows = (pl.ds(rows, 1), pl.ds(0, 1)) if dr else (pl.ds(0, rows), pl.ds(0, rows))
            parts.append((dr, dc) + net.halo(
                dr, dc,
                act.at[:, src_rows, :, pl.ds(0, TILE), :],
                act.at[:, dst_rows, :, pl.ds(cols, TILE), :],
            ))

    def after():
        lines.append(net.halo(1, 0, center_send, center_recv))
        lines.append(net.halo(1, 0, edge_send, edge_recv))

    total = net.all_sum(group_sums(stat), stats, between, after)
    mean, factor = norm_terms(total, members, gain[...])
    bias = shift[...]

    def change(value, k):
        at = slice(k * lanes, (k + 1) * lanes)
        return silu_norm(value, mean[:, at], factor[:, at], bias[:, at])

    net.pending.extend(wait_send for wait_send, _ in lines)
    for _, _, wait_send, _ in parts:
        wait_send()

    @pl.loop(0, frames)
    def _(t):
        for r in range(rows):
            for k in range(blocks):
                act[t, r, k, pl.ds(0, cols), :] = change(act[t, r, k, pl.ds(0, cols), :], k)

    def border(dr, dc, finish):
        at = pl.ds(cols, TILE) if dc else pl.ds(0, cols)
        size = TILE if dc else cols
        places = [rows] if dr else list(range(rows))
        there = net.exists(dr, dc)

        @pl.when(there)
        def _():
            finish()

            @pl.loop(0, frames)
            def _(t):
                for r in places:
                    for k in range(blocks):
                        if dc:
                            value = act[t, r, k, at, :]
                        else:
                            value = edge_recv[t, :, pl.ds(k * lanes, lanes)].astype(F32)
                            value = value + center_recv[0:1, pl.ds(k * lanes, lanes)]
                        act[t, r, k, at, :] = change(value, k)

        @pl.when(jnp.logical_not(there))
        def _():
            @pl.loop(0, frames)
            def _(t):
                for r in places:
                    for k in range(blocks):
                        act[t, r, k, at, :] = jnp.zeros((size, lanes), F32)

    border(1, 0, lambda: [wait_recv() for _, wait_recv in lines])
    for dr, dc, _, wait_recv in parts:
        border(dr, dc, wait_recv)
    gather_halved(act, halved)


def fill(buf, t, values, row_send):
    frames, high, wide, channels = buf.shape
    rows, cols = high - 2, wide - 2 * TILE
    for r in range(rows):
        value = values[r * cols : (r + 1) * cols].astype(BF16)
        buf[t, r + 1, pl.ds(TILE, cols), :] = value.astype(F32)
        if r == rows - 1:
            row_send[0, t] = value
        if r == 0:
            row_send[1, t] = value


def kernel(
    row_peers, col_peers,
    x, k1, d1, k2, d2, k3, g1, s1, g2, s2, g3, s3, out,
    xv, w1, pair1, v1, w2, v2, w3,
    buf1, taps1, act1, half1, slots1, edge1, edged1, center1, centered1,
    buf2, taps2, act2, half2, sends2, slots2, edge2, edged2, center2, centered2,
    buf3, taps3, sends3, slots3,
    stat1, own1, part1, fa1, sa1, stat2, own2, part2, fa2, sa2, stat3, own3, part3, fa3, sa3,
    load, send, recv,
):
    net = Net(row_peers, col_peers, send, recv)
    frames, rows, cols, c1 = x.shape
    latent = k3.shape[2]
    loads = [
        pltpu.make_async_copy(x, xv, load.at[0]),
        pltpu.make_async_copy(k1, w1, load.at[1]),
        pltpu.make_async_copy(k1.at[1], pair1.at[:, pl.ds(0, c1)], load.at[2]),
        pltpu.make_async_copy(k1.at[2], pair1.at[:, pl.ds(c1, c1)], load.at[3]),
        pltpu.make_async_copy(d1, v1, load.at[4]),
        pltpu.make_async_copy(k2, w2, load.at[5]),
        pltpu.make_async_copy(d2, v2, load.at[6]),
    ]
    for a in range(3):
        loads.append(pltpu.make_async_copy(k3.at[a], w3.at[:, pl.ds(a * latent, latent), :], load.at[7 + a]))
    for copy in loads:
        copy.start()
    for buf in (buf1, buf2, buf3):
        clear_rim(buf)
    arrive = net.greet()
    loads[0].wait()

    @pl.loop(0, frames)
    def _(t):
        for r in range(rows):
            buf1[t, r + 1, pl.ds(TILE, cols), :] = xv[t, r].astype(F32)

    places = float(frames * rows * cols * row_peers * col_peers)
    held = []
    beside = lambda parts: [part for part in parts if part[0] == 0]
    beyond = lambda parts: [part for part in parts if part[0] != 0]

    def rim_cols1():
        arrive()
        held.extend(start_rim(net, buf1, (x.at[:, rows - 1], x.at[:, 0]), slots1))
        finish_rim(net, buf1, slots1, beside(held))

    def ready1():
        for copy in loads[1:4]:
            copy.wait()

    within = [(1, rows - 2, EDGE, cols - 2 * EDGE)]
    strips = [(1, rows - 2, 0, EDGE), (1, rows - 2, cols - EDGE, EDGE)]
    level(
        net, buf1, taps1, w1, pair1, (within, strips, [(0, 1, 0, cols), (rows - 1, 1, 0, cols)]),
        act1, half1, (edge1, edged1, center1, centered1), stat1, (own1, part1, fa1, sa1),
        places * (c1 // GROUPS), g1, s1, ready1,
        rim_cols1, lambda: finish_rim(net, buf1, slots1, beyond(held)),
    )
    loads[4].wait()

    @pl.loop(0, frames)
    def _(t):
        fill(buf2, t, product(half1[t], v1[...]), sends2)

    parts = start_rim(net, buf2, (sends2.at[0], sends2.at[1]), slots2)
    c2, c3 = v1.shape[1], v2.shape[1]
    rows2, cols2 = buf2.shape[1] - 2, buf2.shape[2] - 2 * TILE
    level(
        net, buf2, taps2, w2, None,
        ([], [], [(0, rows2, 0, cols2)]),
        act2, half2, (edge2, edged2, center2, centered2), stat2, (own2, part2, fa2, sa2),
        places / 4 * (c2 // GROUPS), g2, s2, loads[5].wait,
        lambda: finish_rim(net, buf2, slots2, beside(parts)),
        lambda: finish_rim(net, buf2, slots2, beyond(parts)),
    )
    loads[6].wait()
    stat3[...] = jnp.zeros_like(stat3)

    @pl.loop(0, frames)
    def _(t):
        value = product(half2[t], v2[...])
        fill(buf3, t, value, sends3)
        value = value.astype(BF16).astype(F32)
        stat3[0:1] += jnp.sum(value, axis=0, keepdims=True)
        stat3[1:2] += jnp.sum(value * value, axis=0, keepdims=True)

    rims = start_rim(net, buf3, (sends3.at[0], sends3.at[1]), slots3)
    total = net.all_sum(group_sums(stat3), (own3, part3, fa3, sa3))
    mean, factor = norm_terms(total, places / 16 * (c3 // GROUPS), g3[...])
    bias = s3[...]
    change = lambda value: silu_norm(value, mean, factor, bias)
    for dr, dc, wait_send, _ in rims:
        net.pending.append(wait_send) if dc == 0 else wait_send()
    rows3, cols3 = buf3.shape[1] - 2, buf3.shape[2] - 2 * TILE

    @pl.loop(0, frames)
    def _(t):
        for r in range(rows3):
            at = pl.ds(TILE, cols3)
            buf3[t, r + 1, at, :] = change(buf3[t, r + 1, at, :])

    finish_rim(net, buf3, slots3, rims, change)

    @pl.loop(0, frames)
    def _(t):
        for r in range(rows3 + 2):
            for e in range(3):
                value = buf3[t, r, pl.ds(TILE - 1 + e, cols3), :]
                for b in range(3):
                    if 0 <= r - b < rows3:
                        taps3[t, pl.ds((r - b) * cols3, cols3), pl.ds((3 * b + e) * c3, c3)] = value

    for copy in loads[7:]:
        copy.wait()
    total = None
    for tap in range(9):
        left = taps3[:, :, pl.ds(tap * c3, c3)].reshape(-1, c3).astype(BF16)
        term = lax.dot_general(left, w3[tap], (((1,), (1,)), ((), ())), preferred_element_type=F32)
        total = term if total is None else total + term
    size = rows3 * cols3
    ages = [
        [total[t * size : (t + 1) * size, a * latent : (a + 1) * latent] for t in range(frames)]
        for a in range(3)
    ]
    for t in range(frames):
        value = ages[0][max(t - 2, 0)] + ages[1][max(t - 1, 0)] + ages[2][t]
        for r in range(rows3):
            out[t, r] = value[r * cols3 : (r + 1) * cols3].astype(BF16)
    for wait in net.pending:
        wait()


def shards(row_peers, col_peers, x, k1, d1, k2, d2, k3, g1, s1, g2, s2, g3, s3):
    frames, rows, cols, c1 = x.shape
    c2, c3, latent = d1.shape[3], d2.shape[3], k3.shape[4]
    channels = (c1, c2, c3)
    shapes = [(rows >> i, cols >> i) for i in range(3)]
    flat3 = lambda k: k.reshape(3, 9 * k.shape[3], k.shape[4])
    flat2 = lambda k: k.reshape(9 * k.shape[2], k.shape[3])
    k3 = jnp.swapaxes(k3, 3, 4).reshape(3, 9, latent, c3)
    weights = (flat3(k1), flat2(d1), flat3(k2), flat2(d2), k3)
    k1f, d1f, k2f, d2f, _ = weights

    def padded(i):
        h, w = shapes[i]
        return pltpu.VMEM((frames, h + 2, w + 2 * TILE, channels[i]), F32)

    def taps(i):
        h, w = shapes[i]
        return pltpu.VMEM((frames, h, w, 9 * channels[i]), BF16)

    def last_taps():
        h, w = shapes[2]
        return pltpu.VMEM((frames, h * w, 9 * channels[2]), F32)

    def center(i):
        return pltpu.VMEM((TILE, channels[i]), F32)

    def edge(i):
        return pltpu.VMEM((frames, shapes[i][1], channels[i]), BF16)

    def act(i):
        h, w = shapes[i]
        return pltpu.VMEM((frames, h + 1, channels[i] // LANES, w + TILE, LANES), F32)

    def half(i):
        h, w = shapes[i + 1]
        return pltpu.VMEM((frames, h * w, 9 * channels[i]), packed_type(w))

    def lines(i):
        return pltpu.VMEM((2, frames, shapes[i][1], channels[i]), BF16)

    def stats(i):
        c = channels[i]
        return [
            pltpu.VMEM((TILE, c), F32),
            pltpu.VMEM((2, LANES), F32),
            pltpu.VMEM((2, LANES), F32),
            pltpu.VMEM((col_peers - 1, 2, LANES), F32),
            pltpu.VMEM((row_peers - 1, 2, LANES), F32),
        ]

    count = copies_needed(row_peers, col_peers)
    scratch = [
        pltpu.VMEM(x.shape, BF16),
        pltpu.VMEM(k1f.shape, BF16),
        pltpu.VMEM((k1f.shape[1], 2 * c1), BF16),
        pltpu.VMEM(d1f.shape, BF16),
        pltpu.VMEM(k2f.shape, BF16),
        pltpu.VMEM(d2f.shape, BF16),
        pltpu.VMEM((9, 3 * latent, c3), BF16),
        padded(0), taps(0), act(0), half(0), lines(0), edge(0), edge(0), center(0), center(0),
        padded(1), taps(1), act(1), half(1), lines(1), lines(1), edge(1), edge(1), center(1), center(1),
        padded(2), last_taps(), lines(2), lines(2),
        *stats(0), *stats(1), *stats(2),
        pltpu.SemaphoreType.DMA((10,)),
        pltpu.SemaphoreType.DMA((count,)),
        pltpu.SemaphoreType.DMA((count,)),
    ]
    anywhere = pl.BlockSpec(memory_space=pl.ANY)
    local = pl.BlockSpec(memory_space=pltpu.VMEM)
    wide = lambda v: v.reshape(1, -1)
    return pl.pallas_call(
        functools.partial(kernel, row_peers, col_peers),
        out_shape=jax.ShapeDtypeStruct((frames, *shapes[2], latent), BF16),
        in_specs=[anywhere] * 6 + [local] * 6,
        out_specs=local,
        scratch_shapes=scratch,
        compiler_params=pltpu.CompilerParams(
            collective_id=0, has_side_effects=True, vmem_limit_bytes=64000 * 1024
        ),
    )(x, *weights, *map(wide, (g1, s1, g2, s2, g3, s3)))


def solution(mesh):
    block = P(None, "rows", "cols", None)
    body = functools.partial(shards, mesh.shape["rows"], mesh.shape["cols"])
    return jax.shard_map(
        body, mesh=mesh, in_specs=(block,) + (P(),) * 11, out_specs=block, check_vma=False
    )
```
